32 devices in a mesh: dp: 8 (over z, y), seq: 4 (over x, core).
Axes of the slice: x: 2, y: 2, z: 4, core: 2. Of those that a mesh axis runs over, the one named last changes fastest.
Arguments:
- tokens: bfloat16 [64, 512, 768], P('dp', 'seq'), may hold values from -12 to 12
- cotangent: bfloat16 [64, 512, 768], P('dp', 'seq'), may hold values from -6 to 6
- lengths: int32 [64], P('dp'), may hold values from 128 to 512, as said below
- mlm_mask: int32 [64, 512], P('dp', 'seq'), may hold values from 0 to 1, as said below
- token_weight: int32 [64, 512], P('dp', 'seq'), may hold values from 1 to 4
- pos_table: bfloat16 [512, 768], P('seq'), may hold values from -4 to 4
- w_qkv: bfloat16 [768, 2304], replicated, may hold values from -0.21875 to 0.21875
- b_query: bfloat16 [768], replicated, may hold values from -4 to 4
- b_value: bfloat16 [768], replicated, may hold values from -4 to 4
- w_out: bfloat16 [768, 768], replicated, may hold values from -0.875 to 0.875
- b_out: bfloat16 [768], replicated, may hold values from -4 to 4
- gain_attn: bfloat16 [768], replicated, may hold values from 0.5 to 1.5
- shift_attn: bfloat16 [768], replicated, may hold values from -4 to 4
- w_up: bfloat16 [768, 3072], replicated, may hold values from -0.21875 to 0.21875
- b_up: bfloat16 [3072], replicated, may hold values from -4 to 4
- w_down: bfloat16 [3072, 768], replicated, may hold values from -0.109375 to 0.109375
- b_down: bfloat16 [768], replicated, may hold values from -4 to 4
- gain_out: bfloat16 [768], replicated, may hold values from 0.5 to 1.5
- shift_out: bfloat16 [768], replicated, may hold values from -4 to 4
Outputs:
- mixed_out: bfloat16 [64, 512, 768], P('dp', 'seq')
- grad_tokens: bfloat16 [64, 512, 768], P('dp', 'seq')
- norm_values: float32 [5], replicated
- grad_pos_table: float32 [512, 768], P('seq', 'dp')
- grad_w_qkv: float32 [768, 2304], P(('dp', 'seq'))
- grad_b_query: float32 [768], P(('dp', 'seq'))
- grad_b_value: float32 [768], P(('dp', 'seq'))
- grad_w_out: float32 [768, 768], P(('dp', 'seq'))
- grad_b_out: float32 [768], P(('dp', 'seq'))
- grad_gain_attn: float32 [768], P(('dp', 'seq'))
- grad_shift_attn: float32 [768], P(('dp', 'seq'))
- grad_w_up: float32 [768, 3072], P(('dp', 'seq'))
- grad_b_up: float32 [3072], P(('dp', 'seq'))
- grad_w_down: float32 [3072, 768], P(('dp', 'seq'))
- grad_b_down: float32 [768], P(('dp', 'seq'))
- grad_gain_out: float32 [768], P(('dp', 'seq'))
- grad_shift_out: float32 [768], P(('dp', 'seq'))
The draws below stay inside these ranges and needn't reach their ends.
Inputs may be any that keep to these rules, and one draw needn't show every extreme that they name: `lengths`: positions at or past a sequence's length are padding. `mlm_mask`: 1 marks a token chosen for masked-token prediction; marks on padding do not count.
All inputs are finite; a program needn't handle non-finite values.
Results may differ from the reference program's by a relative error of at most 0.015.
Values may be sent and summed in bfloat16 or wider, within the bound.
No kernel may reach another device: no remote copies, remote signals or barrier semaphores. Data moves between devices by JAX's collectives and lax.ppermute only.
A program may use at most 256 MiB of HBM per device.

```python
import math
import jax
import jax.numpy as jnp
from jax import lax

D = 768
H = 12
FF = 3072
SEQ_LEN = 512
SEQS = 64


def draw_tokens(key, part):
    cell_key = jax.random.fold_in(key, 1)
    rising = jnp.sqrt(1.0 + 2.0 * jnp.arange(SEQS, dtype=jnp.float32) / max(SEQS - 1, 1))
    base_draw = jnp.clip(jax.random.normal(cell_key, (SEQS, SEQ_LEN, D), jnp.float32), -6.0, 6.0)
    return (base_draw * rising[:, None, None]).astype(jnp.bfloat16)


def draw_lengths(key, part):
    base_key, high_key, low_key = jax.random.split(key, 3)
    drawn = jax.random.randint(base_key, (SEQS,), SEQ_LEN // 4, SEQ_LEN + 1)
    full_row = jax.random.randint(high_key, (), 0, SEQS)
    short_row = (full_row + 1 + jax.random.randint(low_key, (), 0, SEQS - 1)) % SEQS
    return drawn.at[full_row].set(SEQ_LEN).at[short_row].set(SEQ_LEN // 4)


def draw_mlm_mask(key, part):
    kind_key, common_key, heavy_key, cell_key, empty_key = jax.random.split(key, 5)
    row_kind = jax.random.randint(kind_key, (SEQS,), 0, 8)
    common = jax.random.randint(common_key, (SEQS,), 80, 200)
    heavy_rate = jax.random.randint(heavy_key, (SEQS,), 450, 650)
    row_rate = jnp.where(row_kind == 0, 0, jnp.where(row_kind == 1, heavy_rate, common))
    row_rate = row_rate.at[jax.random.randint(empty_key, (), 0, SEQS)].set(0)
    cell_draw = jax.random.randint(cell_key, (SEQS, SEQ_LEN), 0, 1000)
    return (cell_draw < row_rate[:, None]).astype(jnp.int32)


def plant(entries, key, smallest, largest):
    spot = [jax.random.randint(jax.random.fold_in(key, axis), (), 0, length) for axis, length in enumerate(entries.shape)]
    longest = entries.shape.index(max(entries.shape))
    neighbour = spot[:longest] + [(spot[longest] + 1) % entries.shape[longest]] + spot[longest + 1:]
    return entries.at[tuple(spot)].set(smallest).at[tuple(neighbour)].set(largest)


def block_levels(own_key, shape, shards, low, largest):
    level, own = 1.0, jax.random.fold_in(own_key, 6)
    for dim, shards_of in shards:
        steps = jnp.exp(jax.random.uniform(jax.random.fold_in(own, dim), (shards_of,), jnp.float32, low / len(shards), largest / len(shards)))
        level = level * jnp.repeat(steps, shape[dim] // shards_of).reshape([-1 if axis == dim else 1 for axis in range(len(shape))])
    return level


def noise(stream_key, dims, width, most, pieces=(), kind=jnp.bfloat16):
    array = jax.random.normal(stream_key, dims, jnp.float32) * width
    if len(pieces) > 0:
        array = block_levels(stream_key, dims, pieces, -0.22, 0.18) * array
    return jnp.clip(array, min=-most, max=most).astype(kind)


def setup_inputs(seed: int = 0) -> dict:
    key_list = jax.random.split(jax.random.key(seed), 20)
    tokens = draw_tokens(jax.random.fold_in(key_list[19], 71), 0)
    cotangent = noise(key_list[1], (SEQS, SEQ_LEN, D), 1.0, 6.0, ((0, 8), (1, 4)))
    lengths = draw_lengths(jax.random.fold_in(key_list[19], 71), 0)
    mlm_mask = draw_mlm_mask(jax.random.fold_in(key_list[19], 71), 0)
    token_weight = plant(jax.random.randint(key_list[4], (SEQS, SEQ_LEN), 1, 5), jax.random.fold_in(key_list[4], 1), 1, 4).astype(jnp.int32)
    pos_table = noise(key_list[5], (SEQ_LEN, D), 0.3, 4.0, ((0, 4),))
    w_qkv = noise(key_list[6], (D, 3 * D), D ** -0.5, 0.21875)
    b_query = noise(key_list[7], (D,), 0.3, 4.0)
    b_value = noise(key_list[8], (D,), 0.3, 4.0)
    w_out = noise(key_list[9], (D, D), (D // 16) ** -0.5, 0.875)
    b_out = noise(key_list[10], (D,), 0.3, 4.0)
    gain_attn = jnp.clip(1.0 + 0.1 * jax.random.normal(key_list[11], (D,), jnp.float32), 0.5, 1.5).astype(jnp.bfloat16)
    shift_attn = noise(key_list[12], (D,), 0.3, 4.0)
    w_up = noise(key_list[13], (D, FF), D ** -0.5, 0.21875)
    b_up = noise(key_list[14], (FF,), 0.3, 4.0)
    w_down = noise(key_list[15], (FF, D), FF ** -0.5, 0.109375)
    b_down = noise(key_list[16], (D,), 0.3, 4.0)
    gain_out = jnp.clip(1.0 + 0.1 * jax.random.normal(key_list[17], (D,), jnp.float32), 0.5, 1.5).astype(jnp.bfloat16)
    shift_out = noise(key_list[18], (D,), 0.3, 4.0)
    return {"tokens": tokens, "cotangent": cotangent, "lengths": lengths, "mlm_mask": mlm_mask, "token_weight": token_weight, "pos_table": pos_table, "w_qkv": w_qkv, "b_query": b_query, "b_value": b_value, "w_out": w_out, "b_out": b_out, "gain_attn": gain_attn, "shift_attn": shift_attn, "w_up": w_up, "b_up": b_up, "w_down": w_down, "b_down": b_down, "gain_out": gain_out, "shift_out": shift_out}


@jax.custom_vjp
def low(v):
    return lax.optimization_barrier(v.astype(jnp.bfloat16)).astype(jnp.float32)

@jax.custom_vjp
def low_back(v):
    return v

def low_keep(v):
    return (low(v), None)

def low_pass(kept, grad):
    return (grad,)

def back_keep(v):
    return (v, None)

def back_low(kept, grad):
    return (low(grad),)
low.defvjp(low_keep, low_pass)
low_back.defvjp(back_keep, back_low)
norm_eps = 1e-12

def matmul(left_side, right_side):
    return jnp.dot(left_side, right_side, precision=lax.Precision.HIGHEST, preferred_element_type=jnp.float32)

def layer_norm(values, gain_in, shift_in):
    row_mean = lax.optimization_barrier(jnp.mean(values, axis=-1, keepdims=True))
    centred = values - row_mean
    spread = lax.optimization_barrier(jnp.mean(centred * centred, axis=-1, keepdims=True))
    return centred * lax.rsqrt(spread + norm_eps) * gain_in + shift_in

def attend_group(block_args):
    query_rows, key_rows, value_rows, key_live = block_args
    score_scale = 1.0 / math.sqrt(query_rows.shape[-1])
    scores = low_back(jnp.einsum('ghqd,ghkd->ghqk', query_rows, key_rows, precision=lax.Precision.HIGHEST) * score_scale)
    scores = jnp.where(key_live[:, None, None, :], scores, -jnp.inf)
    probs = low(jax.nn.softmax(scores, axis=-1))
    return jnp.einsum('ghqk,ghkd->ghqd', probs, value_rows, precision=lax.Precision.HIGHEST)

def attention(query_rows, key_rows, value_rows, key_live):
    group_size = math.gcd(query_rows.shape[0], max(1, 4096 // query_rows.shape[2]))

    def shaped(array_in):
        return array_in.reshape((array_in.shape[0] // group_size, group_size) + array_in.shape[1:])
    stacked_out = lax.map(jax.checkpoint(attend_group), (shaped(query_rows), shaped(key_rows), shaped(value_rows), shaped(key_live)))
    return stacked_out.reshape(query_rows.shape)

def reference(tokens, cotangent, lengths, mlm_mask, token_weight, pos_table, w_qkv, b_query, b_value, w_out, b_out, gain_attn, shift_attn, w_up, b_up, w_down, b_down, gain_out, shift_out):
    seq_count, seq_len, model_width = tokens.shape
    head_count = H
    head_size = model_width // head_count
    positions = jnp.arange(seq_len, dtype=jnp.int32)
    valid_bool = positions[None, :] < lengths[:, None]
    valid_mask = valid_bool.astype(jnp.float32)
    picked = valid_mask * mlm_mask.astype(jnp.float32)
    masked_count = lax.optimization_barrier(jnp.sum(picked, axis=1))
    weighting = valid_mask * token_weight.astype(jnp.float32) * (1.0 + picked * lengths.astype(jnp.float32)[:, None] / jnp.maximum(masked_count, 1.0)[:, None]) * 0.125

    def forward(tokens_f, pos_f, w_qkv_f, b_query_f, b_value_f, w_out_f, b_out_f, gain_attn_f, shift_attn_f, w_up_f, b_up_f, w_down_f, b_down_f, gain_out_f, shift_out_f):
        resid_in = (tokens_f + pos_f[None]).reshape(-1, model_width)
        flat_in = low(resid_in)
        bias_full = jnp.concatenate([b_query_f, jnp.zeros_like(b_query_f), b_value_f])
        projected = low(low_back(matmul(flat_in, w_qkv_f) + bias_full))
        split_heads = projected.reshape(seq_count, seq_len, 3, head_count, head_size).transpose(2, 0, 3, 1, 4)
        context = attention(split_heads[0], split_heads[1], split_heads[2], valid_bool)
        context = low(low_back(context.transpose(0, 2, 1, 3).reshape(-1, model_width)))
        attn_out = low_back(matmul(context, w_out_f) + b_out_f)
        normed_one = layer_norm(resid_in + attn_out, gain_attn_f, shift_attn_f)
        hidden_pre = low_back(matmul(low(normed_one), w_up_f) + b_up_f)
        hidden_act = low(jax.nn.gelu(hidden_pre, approximate=False))
        ffn_out = low_back(matmul(hidden_act, w_down_f) + b_down_f)
        normed_two = layer_norm(normed_one + ffn_out, gain_out_f, shift_out_f)
        flat_valid = valid_mask.reshape(-1, 1)
        squares = jnp.stack([jnp.sum(flat_valid * member * member) for member in (resid_in, normed_one, normed_two, attn_out, ffn_out)])
        return (normed_two.reshape(seq_count, seq_len, model_width), squares)
    floats = [member.astype(jnp.float32) for member in (tokens, pos_table, w_qkv, b_query, b_value, w_out, b_out, gain_attn, shift_attn, w_up, b_up, w_down, b_down, gain_out, shift_out)]
    mixed_out, backward, squares = jax.vjp(forward, *floats, has_aux=True)
    grad_two = cotangent.astype(jnp.float32) * weighting[..., None]
    gradients = backward(grad_two)
    norm_values = jnp.sqrt(squares / (jnp.sum(valid_mask) * model_width))
    return (mixed_out.astype(jnp.bfloat16), gradients[0].astype(jnp.bfloat16), norm_values, gradients[1], gradients[2], gradients[3], gradients[4], gradients[5], gradients[6], gradients[7], gradients[8], gradients[9], gradients[10], gradients[11], gradients[12], gradients[13], gradients[14])
```

```python
import math

import jax
import jax.numpy as jnp
from jax import lax
from jax.experimental import pallas as pl
from jax.experimental.pallas import tpu as pltpu
from jax.sharding import PartitionSpec as P

H = 12
HD = 64
PAIR = 2 * HD
INTERPRET = False


norm_eps = 1e-12
f32 = jnp.float32
bf16 = jnp.bfloat16
NT = (((1,), (1,)), ((), ()))
TN = (((0,), (0,)), ((), ()))
NN = (((1,), (0,)), ((), ()))


def mm(a, b, dims=NN):
    return lax.dot_general(a, b, dims, preferred_element_type=f32)


def probs_of(q, k, bias):
    s = mm(k, q * (1.0 / math.sqrt(HD)), NT) + bias
    e = jnp.exp(s - jnp.max(s, axis=0, keepdims=True))
    return e, 1.0 / jnp.sum(e, axis=0, keepdims=True)


def wide_bias(bias_ref, length):
    bias = bias_ref[0]
    return jnp.concatenate([bias] * (length // 128), axis=1)


def attend_kernel(q_ref, k_ref, v_ref, bias_ref, out_ref):
    bias = wide_bias(bias_ref, q_ref.shape[1])
    parts = []
    for i in range(2):
        cols = slice(i * HD, (i + 1) * HD)
        e, inv = probs_of(q_ref[0, :, cols], k_ref[0, :, cols], bias)
        parts.append(mm(v_ref[0, :, cols], (e * inv).astype(bf16), TN))
    out_ref[0] = jnp.concatenate(parts, axis=0).T.astype(bf16)


def attend_back_kernel(q_ref, k_ref, v_ref, bias_ref, g_ref, dq_ref, dk_ref, dv_ref):
    bias = wide_bias(bias_ref, q_ref.shape[1])
    scale = 1.0 / math.sqrt(HD)
    dq, dk, dv = [], [], []
    for i in range(2):
        cols = slice(i * HD, (i + 1) * HD)
        q, k, v, g = q_ref[0, :, cols], k_ref[0, :, cols], v_ref[0, :, cols], g_ref[0, :, cols]
        e, inv = probs_of(q, k, bias)
        p = e * inv
        t = p * mm(v, g, NT)
        ds = (t - p * jnp.sum(t, axis=0, keepdims=True)).astype(bf16)
        dv.append(mm(p.astype(bf16), g))
        dk.append(mm(ds, q * scale))
        dq.append(mm(k, ds, TN) * scale)
    dq_ref[0] = jnp.concatenate(dq, axis=0).T.astype(bf16)
    dk_ref[0] = jnp.concatenate(dk, axis=1).astype(bf16)
    dv_ref[0] = jnp.concatenate(dv, axis=1).astype(bf16)


def head_specs(length, pairs):
    def spec(off):
        return pl.BlockSpec((1, length, PAIR), lambda b, h: (b, 0, off + h))

    bias = pl.BlockSpec((1, length, 128), lambda b, h: (b, 0, 0))
    return [spec(0), spec(pairs), spec(2 * pairs), bias], spec(0)


def attend(projected, bias):
    rows, length, width = projected.shape
    pairs = width // (3 * PAIR)
    ins, one = head_specs(length, pairs)
    return pl.pallas_call(
        attend_kernel,
        grid=(rows, pairs),
        in_specs=ins,
        out_specs=one,
        out_shape=jax.ShapeDtypeStruct((rows, length, width // 3), bf16),
        interpret=INTERPRET,
        name="attend",
    )(projected, projected, projected, bias)


def attend_back(projected, bias, grad_context):
    rows, length, width = projected.shape
    pairs = width // (3 * PAIR)
    ins, one = head_specs(length, pairs)
    shape = jax.ShapeDtypeStruct((rows, length, width // 3), bf16)
    return pl.pallas_call(
        attend_back_kernel,
        grid=(rows, pairs),
        in_specs=ins + [one],
        out_specs=[one, one, one],
        out_shape=[shape, shape, shape],
        interpret=INTERPRET,
        name="attend_back",
    )(projected, projected, projected, bias, grad_context)


def swap(value, axis, bits):
    size = lax.axis_size(axis)
    return lax.ppermute(value, axis, [(i, i ^ bits) for i in range(size)])


def reduce_halving(values, order):
    dims = []
    for axis in ("dp", "seq"):
        count = lax.axis_size(axis).bit_length() - 1
        dims += [(axis, 1 << b) for b in reversed(range(count))]
    tail = values.shape[1:]
    cur = values.reshape((2,) * len(dims) + tail)
    rest = [d for d in dims if d not in order]
    picked = [d for d in order if d in dims] + rest[::-1]
    for n, step in enumerate(picked):
        at = dims.index(step)
        mine = (lax.axis_index(step[0]) // step[1]) % 2
        keep = lax.dynamic_index_in_dim(cur, mine, at, keepdims=False)
        send = lax.dynamic_index_in_dim(cur, 1 - mine, at, keepdims=False)
        total = keep.astype(f32) + swap(send, step[0], step[1]).astype(f32)
        cur = total if n + 1 == len(picked) else total.astype(values.dtype)
        dims.pop(at)
    return cur


CORE, XBIT = ("seq", 1), ("seq", 2)
YBIT, ZLOW, ZHIGH = ("dp", 1), ("dp", 2), ("dp", 4)
BY_Y = (CORE, YBIT, ZLOW, XBIT, ZHIGH)
BY_Z = (CORE, ZLOW, YBIT, ZHIGH, XBIT)
BY_X = (CORE, XBIT, YBIT, ZLOW, ZHIGH)


def to_sequences(value, shards, me):
    group = value.shape[0] // shards

    def block(r):
        return lax.dynamic_slice_in_dim(value, (me ^ r) * group, group, 0)

    parts = [block(0)] + [swap(block(r), "seq", r) for r in range(1, shards)]
    return parts


def to_positions(value, shards, me, rows):
    group, length = value.shape[:2]
    span = length // shards
    out = jnp.zeros((rows, span) + value.shape[2:], value.dtype)
    for r in range(shards):
        part = value[:, r * span : (r + 1) * span]
        if r:
            part = swap(part, "seq", r)
        out = lax.dynamic_update_slice_in_dim(out, part, (me ^ r) * group, 0)
    return out


def normalize(values):
    centred = values - jnp.mean(values, axis=-1, keepdims=True)
    spread = lax.rsqrt(jnp.mean(centred * centred, axis=-1, keepdims=True) + norm_eps)
    return centred * spread, spread


def normalize_back(grad, normed, spread, gain):
    scaled = grad * gain
    return spread * (
        scaled
        - jnp.mean(scaled, axis=-1, keepdims=True)
        - normed * jnp.mean(scaled * normed, axis=-1, keepdims=True)
    )


def local(
    tokens,
    cotangent,
    lengths,
    mlm_mask,
    token_weight,
    pos_table,
    w_qkv,
    b_query,
    b_value,
    w_out,
    b_out,
    gain_attn,
    shift_attn,
    w_up,
    b_up,
    w_down,
    b_down,
    gain_out,
    shift_out,
):
    rows, span, width = tokens.shape
    shards = lax.axis_size("seq")
    devices = shards * lax.axis_size("dp")
    me = lax.axis_index("seq")
    group = rows // shards
    length = span * shards
    count = group * length

    positions = me * span + lax.iota(jnp.int32, span)
    valid_here = (positions[None, :] < lengths[:, None]).astype(f32)
    resid_here = tokens.astype(f32) + pos_table.astype(f32)[None]
    square_in = jnp.sum(valid_here[..., None] * resid_here * resid_here)
    flat_in = jnp.concatenate(to_sequences(resid_here.astype(bf16), shards, me), axis=1)
    cot = jnp.concatenate(to_sequences(cotangent, shards, me), axis=1)
    marks = jnp.concatenate(to_sequences(token_weight * 2 + mlm_mask, shards, me), axis=1)
    my_lengths = lax.dynamic_slice_in_dim(lengths, me * group, group, 0)
    order = jnp.concatenate([(me ^ r) * span + lax.iota(jnp.int32, span) for r in range(shards)])
    live = order[None, :] < my_lengths[:, None]
    valid_mask = live.astype(f32)
    bias = jnp.broadcast_to(
        jnp.where(live, 0.0, -jnp.inf).astype(f32)[..., None], (group, length, 128)
    )
    picked = valid_mask * (marks % 2).astype(f32)
    masked_count = jnp.sum(picked, axis=1, keepdims=True)
    weighting = (
        valid_mask
        * (marks // 2).astype(f32)
        * (1.0 + picked * my_lengths.astype(f32)[:, None] / jnp.maximum(masked_count, 1.0))
        * 0.125
    )
    mask_column = valid_mask.reshape(count, 1)

    flat = flat_in.reshape(count, width)
    bias_full = jnp.concatenate(
        [b_query.astype(f32), jnp.zeros((width,), f32), b_value.astype(f32)]
    )
    projected = (mm(flat, w_qkv) + bias_full).astype(bf16).reshape(group, length, 3 * width)
    context = attend(projected, bias).reshape(count, width)
    attn_out = mm(context, w_out) + b_out.astype(f32)
    n_one, r_one = normalize(flat.astype(f32) + attn_out)
    gain_one = gain_attn.astype(f32)
    normed_one = n_one * gain_one + shift_attn.astype(f32)
    ffn_in = normed_one.astype(bf16)
    hidden_pre = mm(ffn_in, w_up) + b_up.astype(f32)
    below = 0.5 * (1.0 + lax.erf(hidden_pre * math.sqrt(0.5)))
    density = jnp.exp(-0.5 * hidden_pre * hidden_pre) * (1.0 / math.sqrt(2.0 * math.pi))
    hidden_act = (hidden_pre * below).astype(bf16)
    slope = (below + hidden_pre * density).astype(bf16)
    ffn_out = mm(hidden_act, w_down) + b_down.astype(f32)
    n_two, r_two = normalize(normed_one + ffn_out)
    gain_two = gain_out.astype(f32)
    normed_two = n_two * gain_two + shift_out.astype(f32)
    mixed_out = to_positions(
        normed_two.astype(bf16).reshape(group, length, width), shards, me, rows
    )
    norms = jnp.stack(
        [square_in]
        + [jnp.sum(mask_column * m * m) for m in (normed_one, normed_two, attn_out, ffn_out)]
        + [jnp.sum(valid_mask)]
    )

    def spread_rows(g):
        return g.astype(bf16).reshape(devices, g.shape[0] // devices, g.shape[1])

    grad_two = cot.reshape(count, width).astype(f32) * weighting.reshape(count, 1)
    grad_gain_out = jnp.sum(grad_two * n_two, axis=0)
    grad_shift_out = jnp.sum(grad_two, axis=0)
    grad_resid_two = normalize_back(grad_two, n_two, r_two, gain_two)
    grad_ffn = grad_resid_two.astype(bf16)
    grad_b_down = jnp.sum(grad_ffn, axis=0, dtype=f32)
    grad_w_down = reduce_halving(spread_rows(mm(hidden_act, grad_ffn, TN)), BY_Y)
    grad_pre = (mm(grad_ffn, w_down, NT) * slope.astype(f32)).astype(bf16)
    grad_b_up = jnp.sum(grad_pre, axis=0, dtype=f32)
    grad_w_up = reduce_halving(spread_rows(mm(ffn_in, grad_pre, TN)), BY_Z)
    grad_one = grad_resid_two + mm(grad_pre, w_up, NT)
    grad_gain_attn = jnp.sum(grad_one * n_one, axis=0)
    grad_shift_attn = jnp.sum(grad_one, axis=0)
    grad_resid_one = normalize_back(grad_one, n_one, r_one, gain_one)
    grad_attn = grad_resid_one.astype(bf16)
    grad_b_out = jnp.sum(grad_attn, axis=0, dtype=f32)
    grad_w_out = reduce_halving(spread_rows(mm(context, grad_attn, TN)), BY_X)
    grad_context = mm(grad_attn, w_out, NT).astype(bf16).reshape(group, length, width)

    vectors = [
        grad_b_out,
        grad_gain_attn,
        grad_shift_attn,
        grad_b_up,
        grad_b_down,
        grad_gain_out,
        grad_shift_out,
    ]
    packed = [v.reshape(devices, -1) for v in vectors]
    packed.append(jnp.broadcast_to(norms[None], (devices, norms.shape[0])))
    small = reduce_halving(jnp.concatenate(packed, axis=1), BY_X)
    cuts = []
    at = 0
    for v in vectors:
        size = v.shape[0] // devices
        cuts.append(small[at : at + size])
        at += size
    norm_values = jnp.sqrt(small[at : at + 5] / (small[at + 5] * width))

    dq, dk, dv = (
        g.reshape(count, width) for g in attend_back(projected, bias, grad_context)
    )
    dw = [
        reduce_halving(spread_rows(mm(flat, g, TN)), path)
        for g, path in ((dq, BY_X), (dk, BY_Y), (dv, BY_Z))
    ]
    grad_w_qkv = jnp.concatenate(dw, axis=1)
    grad_b_query = jnp.sum(dq, axis=0, dtype=f32)
    grad_b_value = jnp.sum(dv, axis=0, dtype=f32)
    late = jnp.concatenate(
        [grad_b_query.reshape(devices, -1), grad_b_value.reshape(devices, -1)], axis=1
    )
    late = reduce_halving(late, BY_X)
    half = width // devices
    grad_input = grad_resid_one + mm(jnp.concatenate([dq, dk, dv], axis=1), w_qkv, NT)
    grad_input = grad_input.reshape(group, length, width)
    grad_tokens = to_positions(grad_input.astype(bf16), shards, me, rows)
    grad_rows = jnp.sum(grad_input, axis=0)
    own = grad_rows[:span]
    for r in range(1, shards):
        own = own + swap(grad_rows[r * span : (r + 1) * span].astype(bf16), "seq", r).astype(f32)
    pieces = lax.axis_size("dp")
    cur = own.astype(bf16).reshape(span, pieces, width // pieces).transpose(1, 0, 2)
    bits = [1 << b for b in range(pieces.bit_length() - 1)]
    for n, bit in enumerate(bits):
        mine = (lax.axis_index("dp") // bit) % 2
        halves = cur.reshape(cur.shape[0] // 2, 2, span, width // pieces)
        keep = lax.dynamic_index_in_dim(halves, mine, 1, keepdims=False)
        send = lax.dynamic_index_in_dim(halves, 1 - mine, 1, keepdims=False)
        total = keep.astype(f32) + swap(send, "dp", bit).astype(f32)
        cur = total if n + 1 == len(bits) else total.astype(bf16)
    grad_pos = cur.reshape(span, width // pieces)
    return (
        mixed_out,
        grad_tokens,
        norm_values,
        grad_pos,
        grad_w_qkv,
        late[:half],
        late[half:],
        grad_w_out,
        cuts[0],
        cuts[1],
        cuts[2],
        grad_w_up,
        cuts[3],
        grad_w_down,
        cuts[4],
        cuts[5],
        cuts[6],
    )


def solution(mesh):
    in_specs = (
        P("dp", "seq", None),
        P("dp", "seq", None),
        P("dp"),
        P("dp", "seq"),
        P("dp", "seq"),
        P("seq", None),
    ) + (P(),) * 13
    both = ("dp", "seq")
    out_specs = (
        P("dp", "seq", None),
        P("dp", "seq", None),
        P(),
        P("seq", "dp"),
        P(both, None),
        P(both),
        P(both),
        P(both, None),
        P(both),
        P(both),
        P(both),
        P(both, None),
        P(both),
        P(both, None),
        P(both),
        P(both),
        P(both),
    )
    return jax.shard_map(local, mesh=mesh, in_specs=in_specs, out_specs=out_specs, check_vma=False)
```

```python
import math

import jax
import jax.numpy as jnp
from jax import lax
from jax.experimental import pallas as pl
from jax.experimental.pallas import tpu as pltpu
from jax.sharding import PartitionSpec as P

H = 12
HD = 64
PAIR = 2 * HD
INTERPRET = False


norm_eps = 1e-12
f32 = jnp.float32
bf16 = jnp.bfloat16
NT = (((1,), (1,)), ((), ()))
TN = (((0,), (0,)), ((), ()))
NN = (((1,), (0,)), ((), ()))


def mm(a, b, dims=NN):
    return lax.dot_general(a, b, dims, preferred_element_type=f32)


def probs_of(q, k, bias):
    s = mm(k, q * (1.0 / math.sqrt(HD)), NT) + bias
    e = jnp.exp(s - jnp.max(s, axis=0, keepdims=True))
    return e, 1.0 / jnp.sum(e, axis=0, keepdims=True)


def rows_of(ref, cols=slice(None)):
    blocks = [ref[i, 0, :, cols] for i in range(ref.shape[0])]
    return jnp.concatenate(blocks, axis=0)


def put_rows(ref, value, cols=slice(None)):
    span = ref.shape[2]
    for i in range(ref.shape[0]):
        ref[i, 0, :, cols] = value[i * span : (i + 1) * span]


def wide_bias(bias_ref):
    bias = rows_of(bias_ref)
    return jnp.concatenate([bias] * (bias.shape[0] // 128), axis=1)


def attend_kernel(q_ref, k_ref, v_ref, bias_ref, out_ref):
    bias = wide_bias(bias_ref)
    parts = []
    for i in range(2):
        cols = slice(i * HD, (i + 1) * HD)
        e, inv = probs_of(rows_of(q_ref, cols), rows_of(k_ref, cols), bias)
        parts.append(mm(rows_of(v_ref, cols), (e * inv).astype(bf16), TN))
    put_rows(out_ref, jnp.concatenate(parts, axis=0).T.astype(bf16))


def attend_back_kernel(q_ref, k_ref, v_ref, bias_ref, g_ref, out_ref):
    bias = wide_bias(bias_ref)
    scale = 1.0 / math.sqrt(HD)
    dq, dk, dv = [], [], []
    for i in range(2):
        cols = slice(i * HD, (i + 1) * HD)
        q, k, v, g = (rows_of(ref, cols) for ref in (q_ref, k_ref, v_ref, g_ref))
        e, inv = probs_of(q, k, bias)
        p = e * inv
        t = p * mm(v, g, NT)
        ds = (t - p * jnp.sum(t, axis=0, keepdims=True)).astype(bf16)
        dv.append(mm(p.astype(bf16), g))
        dk.append(mm(ds, q * scale))
        dq.append(mm(k, ds, TN) * scale)
    grads = (
        jnp.concatenate(dq, axis=0).T.astype(bf16),
        jnp.concatenate(dk, axis=1).astype(bf16),
        jnp.concatenate(dv, axis=1).astype(bf16),
    )
    pairs = out_ref.shape[3] // (3 * PAIR)
    for j in range(pairs):

        @pl.when(pl.program_id(1) == j)
        def _():
            for part, grad in enumerate(grads):
                at = (part * pairs + j) * PAIR
                put_rows(out_ref, grad, slice(at, at + PAIR))


def pair_spec(shape, off):
    return pl.BlockSpec((shape[0], 1, shape[2], PAIR), lambda b, h: (0, b, 0, off + h))


def bias_spec(shape):
    return pl.BlockSpec((shape[0], 1, shape[2], 128), lambda b, h: (0, b, 0, 0))


def attend(projected, bias):
    shape = projected.shape
    pairs = shape[3] // (3 * PAIR)
    return pl.pallas_call(
        attend_kernel,
        grid=(shape[1], pairs),
        in_specs=[pair_spec(shape, i * pairs) for i in range(3)] + [bias_spec(shape)],
        out_specs=pair_spec(shape, 0),
        out_shape=jax.ShapeDtypeStruct(shape[:3] + (shape[3] // 3,), bf16),
        interpret=INTERPRET,
        name="attend",
    )(projected, projected, projected, bias)


def attend_back(projected, bias, grad_context, first, take):
    shape = projected.shape
    pairs = shape[3] // (3 * PAIR)
    wide = 3 * take * PAIR
    return pl.pallas_call(
        attend_back_kernel,
        grid=(shape[1], take),
        in_specs=[pair_spec(shape, i * pairs + first) for i in range(3)]
        + [bias_spec(shape), pair_spec(shape, first)],
        out_specs=pl.BlockSpec((shape[0], 1, shape[2], wide), lambda b, h: (0, b, 0, 0)),
        out_shape=jax.ShapeDtypeStruct(shape[:3] + (wide,), bf16),
        interpret=INTERPRET,
        name="attend_back",
    )(projected, projected, projected, bias, grad_context)


def swap(value, axis, bits):
    size = lax.axis_size(axis)
    return lax.ppermute(value, axis, [(i, i ^ bits) for i in range(size)])


class Halving:
    def __init__(self, values, order):
        dims = []
        for axis in ("dp", "seq"):
            count = lax.axis_size(axis).bit_length() - 1
            dims += [(axis, 1 << b) for b in reversed(range(count))]
        self.cur = values.reshape((2,) * len(dims) + values.shape[1:])
        self.dims = dims
        self.left = [d for d in order if d in dims] + [d for d in dims[::-1] if d not in order]

    def step(self):
        if not self.left:
            return
        bit = self.left.pop(0)
        at = self.dims.index(bit)
        self.dims.pop(at)
        mine = (lax.axis_index(bit[0]) // bit[1]) % 2
        keep = lax.dynamic_index_in_dim(self.cur, mine, at, keepdims=False)
        send = lax.dynamic_index_in_dim(self.cur, 1 - mine, at, keepdims=False)
        total = keep.astype(f32) + swap(send, bit[0], bit[1]).astype(f32)
        self.cur = total.astype(self.cur.dtype) if self.left else total

    def finish(self):
        while self.left:
            self.step()
        return self.cur


def tie(value, *chains):
    value, held = lax.optimization_barrier((value, [c.cur for c in chains]))
    for chain, cur in zip(chains, held):
        chain.cur = cur
        chain.step()
    return value


CORE, XBIT = ("seq", 1), ("seq", 2)
YBIT, ZLOW, ZHIGH = ("dp", 1), ("dp", 2), ("dp", 4)
DOWN_PATH = (CORE, YBIT, XBIT, ZLOW, ZHIGH)
UP_PATH = (CORE, ZLOW, YBIT, ZHIGH, XBIT)
OUT_PATH = (CORE, XBIT, YBIT, ZLOW, ZHIGH)
HEAD_PATH = (CORE, YBIT, ZLOW, XBIT, ZHIGH)
LAST_PATH = (CORE, ZLOW, YBIT, XBIT, ZHIGH)


def to_sequences(value, shards, me):
    group = value.shape[0] // shards

    def block(r):
        return lax.dynamic_slice_in_dim(value, (me ^ r) * group, group, 0)

    parts = [block(0)] + [swap(block(r), "seq", r) for r in range(1, shards)]
    return jnp.concatenate(parts, axis=0)


def send_back(value):
    return [value[0]] + [swap(value[r], "seq", r) for r in range(1, value.shape[0])]


def to_positions(parts, me):
    group = parts[0].shape[0]
    out = jnp.zeros((group * len(parts),) + parts[0].shape[1:], parts[0].dtype)
    for r, part in enumerate(parts):
        out = lax.dynamic_update_slice_in_dim(out, part, (me ^ r) * group, 0)
    return out


def normalize(values):
    centred = values - jnp.mean(values, axis=-1, keepdims=True)
    spread = lax.rsqrt(jnp.mean(centred * centred, axis=-1, keepdims=True) + norm_eps)
    return centred * spread, spread


def normalize_back(grad, normed, spread, gain):
    scaled = grad * gain
    return spread * (
        scaled
        - jnp.mean(scaled, axis=-1, keepdims=True)
        - normed * jnp.mean(scaled * normed, axis=-1, keepdims=True)
    )


def local(
    tokens,
    cotangent,
    lengths,
    mlm_mask,
    token_weight,
    pos_table,
    w_qkv,
    b_query,
    b_value,
    w_out,
    b_out,
    gain_attn,
    shift_attn,
    w_up,
    b_up,
    w_down,
    b_down,
    gain_out,
    shift_out,
):
    rows, span, width = tokens.shape
    shards = lax.axis_size("seq")
    devices = shards * lax.axis_size("dp")
    me = lax.axis_index("seq")
    group = rows // shards
    count = group * span * shards

    positions = me * span + lax.iota(jnp.int32, span)
    valid_here = (positions[None, :] < lengths[:, None]).astype(f32)
    resid_here = tokens.astype(f32) + pos_table.astype(f32)[None]
    square_in = jnp.sum(valid_here[..., None] * resid_here * resid_here)
    flat = to_sequences(resid_here.astype(bf16), shards, me).reshape(count, width)
    marks = to_sequences(token_weight * 2 + mlm_mask, shards, me).reshape(shards, group, span)
    flat, cotangent = lax.optimization_barrier((flat, cotangent))
    cot = to_sequences(cotangent, shards, me)
    my_lengths = lax.dynamic_slice_in_dim(lengths, me * group, group, 0)
    order = jnp.stack([(me ^ r) * span + lax.iota(jnp.int32, span) for r in range(shards)])
    live = order[:, None, :] < my_lengths[None, :, None]
    valid_mask = live.astype(f32)
    bias = jnp.broadcast_to(
        jnp.where(live, 0.0, -jnp.inf).astype(f32)[..., None], (shards, group, span, 128)
    )
    picked = valid_mask * (marks % 2).astype(f32)
    masked_count = jnp.sum(picked, axis=(0, 2), keepdims=True)
    weighting = (
        valid_mask
        * (marks // 2).astype(f32)
        * (
            1.0
            + picked * my_lengths.astype(f32)[None, :, None] / jnp.maximum(masked_count, 1.0)
        )
        * 0.125
    )
    mask_column = valid_mask.reshape(count, 1)

    bias_full = jnp.concatenate(
        [b_query.astype(f32), jnp.zeros((width,), f32), b_value.astype(f32)]
    )
    projected = (mm(flat, w_qkv) + bias_full).astype(bf16).reshape(shards, group, span, 3 * width)
    context = attend(projected, bias).reshape(count, width)
    attn_out = mm(context, w_out) + b_out.astype(f32)
    n_one, r_one = normalize(flat.astype(f32) + attn_out)
    gain_one = gain_attn.astype(f32)
    normed_one = n_one * gain_one + shift_attn.astype(f32)
    ffn_in = normed_one.astype(bf16)
    hidden_pre = mm(ffn_in, w_up) + b_up.astype(f32)
    below = 0.5 * (1.0 + lax.erf(hidden_pre * math.sqrt(0.5)))
    density = jnp.exp(-0.5 * hidden_pre * hidden_pre) * (1.0 / math.sqrt(2.0 * math.pi))
    hidden_act = (hidden_pre * below).astype(bf16)
    slope = (below + hidden_pre * density).astype(bf16)
    ffn_out = mm(hidden_act, w_down) + b_down.astype(f32)
    n_two, r_two = normalize(normed_one + ffn_out)
    gain_two = gain_out.astype(f32)
    normed_two = n_two * gain_two + shift_out.astype(f32)
    mixed_parts = send_back(normed_two.astype(bf16).reshape(shards, group, span, width))
    norms = jnp.stack(
        [square_in]
        + [jnp.sum(mask_column * m * m) for m in (normed_one, normed_two, attn_out, ffn_out)]
        + [jnp.sum(valid_mask)]
    )

    def spread_rows(g):
        return g.astype(bf16).reshape(devices, g.shape[0] // devices, g.shape[1])

    grad_two = cot.reshape(count, width).astype(f32) * weighting.reshape(count, 1)
    grad_gain_out = jnp.sum(grad_two * n_two, axis=0)
    grad_shift_out = jnp.sum(grad_two, axis=0)
    grad_resid_two = normalize_back(grad_two, n_two, r_two, gain_two)
    grad_ffn = grad_resid_two.astype(bf16)
    grad_b_down = jnp.sum(grad_ffn, axis=0, dtype=f32)
    down_sum = Halving(spread_rows(mm(hidden_act, grad_ffn, TN)), DOWN_PATH)
    grad_ffn = tie(grad_ffn, down_sum)
    grad_pre = (mm(grad_ffn, w_down, NT) * slope.astype(f32)).astype(bf16)
    grad_pre = tie(grad_pre, down_sum)
    grad_b_up = jnp.sum(grad_pre, axis=0, dtype=f32)
    up_sum = Halving(spread_rows(mm(ffn_in, grad_pre, TN)), UP_PATH)
    grad_pre = tie(grad_pre, up_sum)
    grad_one = grad_resid_two + mm(grad_pre, w_up, NT)
    grad_one = tie(grad_one, up_sum)
    grad_gain_attn = jnp.sum(grad_one * n_one, axis=0)
    grad_shift_attn = jnp.sum(grad_one, axis=0)
    grad_resid_one = normalize_back(grad_one, n_one, r_one, gain_one)
    grad_attn = grad_resid_one.astype(bf16)
    grad_b_out = jnp.sum(grad_attn, axis=0, dtype=f32)
    out_sum = Halving(spread_rows(mm(context, grad_attn, TN)), OUT_PATH)
    grad_context = mm(grad_attn, w_out, NT).astype(bf16).reshape(shards, group, span, width)
    grad_context, mixed_parts = lax.optimization_barrier((grad_context, mixed_parts))
    mixed_out = to_positions(mixed_parts, me)
    grad_context = tie(grad_context, down_sum, out_sum)

    pairs = width // PAIR
    takes = (pairs - pairs // 3, pairs // 3)
    first = attend_back(projected, bias, grad_context, 0, takes[0]).reshape(count, -1)
    head_sum = Halving(spread_rows(mm(flat, first, TN)), HEAD_PATH)
    grad_context = tie(grad_context, down_sum, up_sum, out_sum, head_sum)
    last = attend_back(projected, bias, grad_context, takes[0], takes[1]).reshape(count, -1)
    last = tie(last, down_sum, up_sum, out_sum, head_sum)
    first_sum = jnp.sum(first, axis=0, dtype=f32)
    last_sum = jnp.sum(last, axis=0, dtype=f32)

    def split(values, axis):
        return jnp.split(values, 3, axis=axis)

    (q_first, _, v_first), (q_last, _, v_last) = split(first_sum, 0), split(last_sum, 0)
    each = width // devices
    vectors = [
        jnp.concatenate([q_first, q_last]),
        jnp.concatenate([v_first, v_last]),
        grad_b_out,
        grad_gain_attn,
        grad_shift_attn,
        grad_b_down,
        grad_gain_out,
        grad_shift_out,
    ]
    ups = grad_b_up.shape[0] // width
    lines = -(-norms.shape[0] // each)
    norms = jnp.pad(norms, (0, lines * each - norms.shape[0])).reshape(lines, each)
    table = jnp.concatenate(
        [v[None] for v in vectors]
        + [
            grad_b_up.reshape(devices, ups, each).transpose(1, 0, 2).reshape(ups, width),
            jnp.tile(norms, (1, devices)),
        ],
        axis=0,
    )
    table = jnp.pad(table, ((0, 128 - table.shape[0]), (0, 0))).T
    last_grad = jnp.concatenate([mm(flat, last, TN).astype(bf16), table.astype(bf16)], axis=1)
    last_sum = Halving(spread_rows(last_grad), LAST_PATH)
    cut = takes[0] * PAIR

    def columns(lo, hi):
        return [w_qkv[:, i * width + lo : i * width + hi] for i in range(3)]

    w_first = jnp.concatenate(columns(0, cut), axis=1)
    w_last = jnp.concatenate(columns(cut, width), axis=1)
    grad_input = grad_resid_one + mm(first, w_first, NT) + mm(last, w_last, NT)
    grad_input = grad_input.reshape(shards, group, span, width)
    grad_tokens = to_positions(send_back(grad_input.astype(bf16)), me)
    cur = jnp.sum(grad_input, axis=1)
    bit = 1
    while cur.shape[0] > 1:
        halves = cur.reshape(cur.shape[0] // 2, 2, span, width)
        cur = halves[:, 0] + swap(halves[:, 1].astype(bf16), "seq", bit).astype(f32)
        bit *= 2
    pieces = lax.axis_size("dp")
    cur = cur[0].astype(bf16).reshape(span, pieces, width // pieces).transpose(1, 0, 2)
    bits = [1 << b for b in range(pieces.bit_length() - 1)]
    for n, bit in enumerate(bits):
        mine = (lax.axis_index("dp") // bit) % 2
        halves = cur.reshape(cur.shape[0] // 2, 2, span, width // pieces)
        keep = lax.dynamic_index_in_dim(halves, mine, 1, keepdims=False)
        send = lax.dynamic_index_in_dim(halves, 1 - mine, 1, keepdims=False)
        total = keep.astype(f32) + swap(send, "dp", bit).astype(f32)
        cur = total if n + 1 == len(bits) else total.astype(bf16)
    grad_pos = cur.reshape(span, width // pieces)

    grad_w_down = down_sum.finish()
    grad_w_up = up_sum.finish()
    grad_w_out = out_sum.finish()
    head_part = split(head_sum.finish(), 1)
    last_part = last_sum.finish()
    small = last_part[:, last.shape[1] :].T
    last_part = split(last_part[:, : last.shape[1]], 1)
    grad_w_qkv = jnp.concatenate([x for pair in zip(head_part, last_part) for x in pair], axis=1)
    rest = len(vectors)
    wide_up = small[rest : rest + ups].reshape(-1)
    norms = small[rest + ups : rest + ups + lines].reshape(-1)
    norm_values = jnp.sqrt(norms[:5] / (norms[5] * width))
    return (
        mixed_out,
        grad_tokens,
        norm_values,
        grad_pos,
        grad_w_qkv,
        small[0],
        small[1],
        grad_w_out,
        small[2],
        small[3],
        small[4],
        grad_w_up,
        wide_up,
        grad_w_down,
        small[5],
        small[6],
        small[7],
    )


def solution(mesh):
    in_specs = (
        P("dp", "seq", None),
        P("dp", "seq", None),
        P("dp"),
        P("dp", "seq"),
        P("dp", "seq"),
        P("seq", None),
    ) + (P(),) * 13
    both = ("dp", "seq")
    out_specs = (
        P("dp", "seq", None),
        P("dp", "seq", None),
        P(),
        P("seq", "dp"),
        P(both, None),
        P(both),
        P(both),
        P(both, None),
        P(both),
        P(both),
        P(both),
        P(both, None),
        P(both),
        P(both, None),
        P(both),
        P(both),
        P(both),
    )
    return jax.shard_map(local, mesh=mesh, in_specs=in_specs, out_specs=out_specs, check_vma=False)
```

```python
import math

import jax
import jax.numpy as jnp
from jax import lax
from jax.experimental import pallas as pl
from jax.experimental.pallas import tpu as pltpu
from jax.sharding import PartitionSpec as P

H = 12
HD = 64
PAIR = 2 * HD
INTERPRET = False


norm_eps = 1e-12
f32 = jnp.float32
bf16 = jnp.bfloat16
NT = (((1,), (1,)), ((), ()))
TN = (((0,), (0,)), ((), ()))
NN = (((1,), (0,)), ((), ()))


def mm(a, b, dims=NN):
    return lax.dot_general(a, b, dims, preferred_element_type=f32)


def probs_of(q, k, bias):
    s = mm(k, q * (1.0 / math.sqrt(HD)), NT) + bias
    e = jnp.exp(s - jnp.max(s, axis=0, keepdims=True))
    return e, 1.0 / jnp.sum(e, axis=0, keepdims=True)


def rows_of(ref, cols=slice(None)):
    blocks = [ref[i, 0, :, cols] for i in range(ref.shape[0])]
    return jnp.concatenate(blocks, axis=0)


def put_rows(ref, value, cols=slice(None)):
    span = ref.shape[2]
    for i in range(ref.shape[0]):
        ref[i, 0, :, cols] = value[i * span : (i + 1) * span]


def wide_bias(bias_ref):
    bias = rows_of(bias_ref)
    return jnp.concatenate([bias] * (bias.shape[0] // 128), axis=1)


def attend_kernel(q_ref, k_ref, v_ref, bias_ref, out_ref):
    bias = wide_bias(bias_ref)
    parts = []
    for i in range(2):
        cols = slice(i * HD, (i + 1) * HD)
        e, inv = probs_of(rows_of(q_ref, cols), rows_of(k_ref, cols), bias)
        parts.append(mm(rows_of(v_ref, cols), (e * inv).astype(bf16), TN))
    put_rows(out_ref, jnp.concatenate(parts, axis=0).T.astype(bf16))


def attend_back_kernel(q_ref, k_ref, v_ref, bias_ref, g_ref, out_ref):
    bias = wide_bias(bias_ref)
    scale = 1.0 / math.sqrt(HD)
    dq, dk, dv = [], [], []
    for i in range(2):
        cols = slice(i * HD, (i + 1) * HD)
        q, k, v, g = (rows_of(ref, cols) for ref in (q_ref, k_ref, v_ref, g_ref))
        e, inv = probs_of(q, k, bias)
        p = e * inv
        t = p * mm(v, g, NT)
        ds = (t - p * jnp.sum(t, axis=0, keepdims=True)).astype(bf16)
        dv.append(mm(p.astype(bf16), g))
        dk.append(mm(ds, q * scale))
        dq.append(mm(k, ds, TN) * scale)
    grads = (
        jnp.concatenate(dq, axis=0).T.astype(bf16),
        jnp.concatenate(dk, axis=1).astype(bf16),
        jnp.concatenate(dv, axis=1).astype(bf16),
    )
    pairs = out_ref.shape[3] // (3 * PAIR)
    for j in range(pairs):

        @pl.when(pl.program_id(1) == j)
        def _():
            for part, grad in enumerate(grads):
                at = (part * pairs + j) * PAIR
                put_rows(out_ref, grad, slice(at, at + PAIR))


def pair_spec(shape, off):
    return pl.BlockSpec((shape[0], 1, shape[2], PAIR), lambda b, h: (0, b, 0, off + h))


def bias_spec(shape):
    return pl.BlockSpec((shape[0], 1, shape[2], 128), lambda b, h: (0, b, 0, 0))


def attend(projected, bias):
    shape = projected.shape
    pairs = shape[3] // (3 * PAIR)
    return pl.pallas_call(
        attend_kernel,
        grid=(shape[1], pairs),
        in_specs=[pair_spec(shape, i * pairs) for i in range(3)] + [bias_spec(shape)],
        out_specs=pair_spec(shape, 0),
        out_shape=jax.ShapeDtypeStruct(shape[:3] + (shape[3] // 3,), bf16),
        interpret=INTERPRET,
        name="attend",
    )(projected, projected, projected, bias)


def attend_back(projected, bias, grad_context, first, take):
    shape = projected.shape
    pairs = shape[3] // (3 * PAIR)
    wide = 3 * take * PAIR
    return pl.pallas_call(
        attend_back_kernel,
        grid=(shape[1], take),
        in_specs=[pair_spec(shape, i * pairs + first) for i in range(3)]
        + [bias_spec(shape), pair_spec(shape, first)],
        out_specs=pl.BlockSpec((shape[0], 1, shape[2], wide), lambda b, h: (0, b, 0, 0)),
        out_shape=jax.ShapeDtypeStruct(shape[:3] + (wide,), bf16),
        interpret=INTERPRET,
        name="attend_back",
    )(projected, projected, projected, bias, grad_context)


def swap(value, axis, bits):
    size = lax.axis_size(axis)
    return lax.ppermute(value, axis, [(i, i ^ bits) for i in range(size)])


class Halving:
    def __init__(self, values, order):
        dims = []
        for axis in ("dp", "seq"):
            count = lax.axis_size(axis).bit_length() - 1
            dims += [(axis, 1 << b) for b in reversed(range(count))]
        self.cur = values.reshape((2,) * len(dims) + values.shape[1:])
        self.dims = dims
        self.left = [d for d in order if d in dims] + [d for d in dims[::-1] if d not in order]

    def step(self):
        if not self.left:
            return
        bit = self.left.pop(0)
        at = self.dims.index(bit)
        self.dims.pop(at)
        mine = (lax.axis_index(bit[0]) // bit[1]) % 2
        keep = lax.dynamic_index_in_dim(self.cur, mine, at, keepdims=False)
        send = lax.dynamic_index_in_dim(self.cur, 1 - mine, at, keepdims=False)
        total = keep.astype(f32) + swap(send, bit[0], bit[1]).astype(f32)
        self.cur = total.astype(self.cur.dtype) if self.left else total

    def finish(self):
        while self.left:
            self.step()
        return self.cur


def tie(value, *chains):
    value, held = lax.optimization_barrier((value, [c.cur for c in chains]))
    for chain, cur in zip(chains, held):
        chain.cur = cur
        chain.step()
    return value


CORE, XBIT = ("seq", 1), ("seq", 2)
YBIT, ZLOW, ZHIGH = ("dp", 1), ("dp", 2), ("dp", 4)
UP_PATH = (CORE, ZLOW, YBIT, ZHIGH, XBIT)
HEAD_PATH = (CORE, YBIT, ZLOW, XBIT, ZHIGH)
LAST_PATH = (CORE, ZLOW, YBIT, XBIT, ZHIGH)


def to_sequences(value, shards, me):
    group = value.shape[0] // shards

    def block(r):
        return lax.dynamic_slice_in_dim(value, (me ^ r) * group, group, 0)

    parts = [block(0)] + [swap(block(r), "seq", r) for r in range(1, shards)]
    return jnp.concatenate(parts, axis=0)


def send_back(value):
    return [value[0]] + [swap(value[r], "seq", r) for r in range(1, value.shape[0])]


def to_positions(parts, me):
    group = parts[0].shape[0]
    out = jnp.zeros((group * len(parts),) + parts[0].shape[1:], parts[0].dtype)
    for r, part in enumerate(parts):
        out = lax.dynamic_update_slice_in_dim(out, part, (me ^ r) * group, 0)
    return out


def normalize(values):
    centred = values - jnp.mean(values, axis=-1, keepdims=True)
    spread = lax.rsqrt(jnp.mean(centred * centred, axis=-1, keepdims=True) + norm_eps)
    return centred * spread, spread


def normalize_back(grad, normed, spread, gain):
    scaled = grad * gain
    return spread * (
        scaled
        - jnp.mean(scaled, axis=-1, keepdims=True)
        - normed * jnp.mean(scaled * normed, axis=-1, keepdims=True)
    )


def local(
    tokens,
    cotangent,
    lengths,
    mlm_mask,
    token_weight,
    pos_table,
    w_qkv,
    b_query,
    b_value,
    w_out,
    b_out,
    gain_attn,
    shift_attn,
    w_up,
    b_up,
    w_down,
    b_down,
    gain_out,
    shift_out,
):
    rows, span, width = tokens.shape
    shards = lax.axis_size("seq")
    devices = shards * lax.axis_size("dp")
    me = lax.axis_index("seq")
    group = rows // shards
    count = group * span * shards

    positions = me * span + lax.iota(jnp.int32, span)
    valid_here = (positions[None, :] < lengths[:, None]).astype(f32)
    resid_here = tokens.astype(f32) + pos_table.astype(f32)[None]
    square_in = jnp.sum(valid_here[..., None] * resid_here * resid_here)
    flat = to_sequences(resid_here.astype(bf16), shards, me).reshape(count, width)
    marks = to_sequences(token_weight * 2 + mlm_mask, shards, me).reshape(shards, group, span)
    flat, cotangent = lax.optimization_barrier((flat, cotangent))
    cot = to_sequences(cotangent, shards, me)
    my_lengths = lax.dynamic_slice_in_dim(lengths, me * group, group, 0)
    order = jnp.stack([(me ^ r) * span + lax.iota(jnp.int32, span) for r in range(shards)])
    live = order[:, None, :] < my_lengths[None, :, None]
    valid_mask = live.astype(f32)
    bias = jnp.broadcast_to(
        jnp.where(live, 0.0, -jnp.inf).astype(f32)[..., None], (shards, group, span, 128)
    )
    picked = valid_mask * (marks % 2).astype(f32)
    masked_count = jnp.sum(picked, axis=(0, 2), keepdims=True)
    weighting = (
        valid_mask
        * (marks // 2).astype(f32)
        * (
            1.0
            + picked * my_lengths.astype(f32)[None, :, None] / jnp.maximum(masked_count, 1.0)
        )
        * 0.125
    )
    mask_column = valid_mask.reshape(count, 1)

    bias_full = jnp.concatenate(
        [b_query.astype(f32), jnp.zeros((width,), f32), b_value.astype(f32)]
    )
    projected = (mm(flat, w_qkv) + bias_full).astype(bf16).reshape(shards, group, span, 3 * width)
    context = attend(projected, bias).reshape(count, width)
    context, cot = lax.optimization_barrier((context, cot))
    attn_out = mm(context, w_out) + b_out.astype(f32)
    n_one, r_one = normalize(flat.astype(f32) + attn_out)
    gain_one = gain_attn.astype(f32)
    normed_one = n_one * gain_one + shift_attn.astype(f32)
    ffn_in = normed_one.astype(bf16)
    hidden_pre = mm(ffn_in, w_up) + b_up.astype(f32)
    below = 0.5 * (1.0 + lax.erf(hidden_pre * math.sqrt(0.5)))
    density = jnp.exp(-0.5 * hidden_pre * hidden_pre) * (1.0 / math.sqrt(2.0 * math.pi))
    hidden_act = (hidden_pre * below).astype(bf16)
    slope = (below + hidden_pre * density).astype(bf16)
    ffn_out = mm(hidden_act, w_down) + b_down.astype(f32)
    n_two, r_two = normalize(normed_one + ffn_out)
    gain_two = gain_out.astype(f32)
    normed_two = n_two * gain_two + shift_out.astype(f32)
    mixed_parts = send_back(normed_two.astype(bf16).reshape(shards, group, span, width))
    norms = jnp.stack(
        [square_in]
        + [jnp.sum(mask_column * m * m) for m in (normed_one, normed_two, attn_out, ffn_out)]
        + [jnp.sum(valid_mask)]
    )

    def spread_rows(g):
        return g.astype(bf16).reshape(devices, g.shape[0] // devices, g.shape[1])

    grad_two = cot.reshape(count, width).astype(f32) * weighting.reshape(count, 1)
    grad_gain_out = jnp.sum(grad_two * n_two, axis=0)
    grad_shift_out = jnp.sum(grad_two, axis=0)
    grad_resid_two = normalize_back(grad_two, n_two, r_two, gain_two)
    grad_ffn = grad_resid_two.astype(bf16)
    grad_b_down = jnp.sum(grad_ffn, axis=0, dtype=f32)
    down_part = mm(hidden_act, grad_ffn, TN).astype(bf16)
    grad_ffn, down_part = lax.optimization_barrier((grad_ffn, down_part))
    grad_w_down = lax.psum_scatter(down_part, ("dp", "seq"), scatter_dimension=0, tiled=True)
    grad_w_down = grad_w_down.astype(f32)
    grad_pre = (mm(grad_ffn, w_down, NT) * slope.astype(f32)).astype(bf16)
    grad_b_up = jnp.sum(grad_pre, axis=0, dtype=f32)
    up_sum = Halving(spread_rows(mm(ffn_in, grad_pre, TN)), UP_PATH)
    grad_pre = tie(grad_pre, up_sum)
    grad_one = grad_resid_two + mm(grad_pre, w_up, NT)
    grad_one = tie(grad_one, up_sum)
    grad_gain_attn = jnp.sum(grad_one * n_one, axis=0)
    grad_shift_attn = jnp.sum(grad_one, axis=0)
    grad_resid_one = normalize_back(grad_one, n_one, r_one, gain_one)
    grad_attn = grad_resid_one.astype(bf16)
    grad_b_out = jnp.sum(grad_attn, axis=0, dtype=f32)
    out_part = mm(context, grad_attn, TN).astype(bf16)
    grad_context = mm(grad_attn, w_out, NT).astype(bf16).reshape(shards, group, span, width)
    grad_context, mixed_parts = lax.optimization_barrier((grad_context, mixed_parts))
    mixed_out = to_positions(mixed_parts, me)

    pairs = width // PAIR
    takes = (pairs - pairs // 3, pairs // 3)
    first = attend_back(projected, bias, grad_context, 0, takes[0]).reshape(count, -1)
    head_part = jnp.concatenate([mm(flat, first, TN).astype(bf16), out_part], axis=1)
    head_sum = Halving(spread_rows(head_part), HEAD_PATH)
    grad_context = tie(grad_context, up_sum, head_sum)
    last = attend_back(projected, bias, grad_context, takes[0], takes[1]).reshape(count, -1)
    last = tie(last, up_sum, head_sum)
    first_sum = jnp.sum(first, axis=0, dtype=f32)
    last_sum = jnp.sum(last, axis=0, dtype=f32)

    def split(values, axis):
        return jnp.split(values, 3, axis=axis)

    (q_first, _, v_first), (q_last, _, v_last) = split(first_sum, 0), split(last_sum, 0)
    each = width // devices
    vectors = [
        jnp.concatenate([q_first, q_last]),
        jnp.concatenate([v_first, v_last]),
        grad_b_out,
        grad_gain_attn,
        grad_shift_attn,
        grad_b_down,
        grad_gain_out,
        grad_shift_out,
    ]
    ups = grad_b_up.shape[0] // width
    lines = -(-norms.shape[0] // each)
    norms = jnp.pad(norms, (0, lines * each - norms.shape[0])).reshape(lines, each)
    table = jnp.concatenate(
        [v[None] for v in vectors]
        + [
            grad_b_up.reshape(devices, ups, each).transpose(1, 0, 2).reshape(ups, width),
            jnp.tile(norms, (1, devices)),
        ],
        axis=0,
    )
    table = jnp.pad(table, ((0, 128 - table.shape[0]), (0, 0))).T
    last_grad = jnp.concatenate([mm(flat, last, TN).astype(bf16), table.astype(bf16)], axis=1)
    last_sum = Halving(spread_rows(last_grad), LAST_PATH)
    last = tie(last, last_sum)
    cut = takes[0] * PAIR

    def columns(lo, hi):
        return [w_qkv[:, i * width + lo : i * width + hi] for i in range(3)]

    w_first = jnp.concatenate(columns(0, cut), axis=1)
    w_last = jnp.concatenate(columns(cut, width), axis=1)
    grad_input = grad_resid_one + mm(first, w_first, NT) + mm(last, w_last, NT)
    grad_input = tie(grad_input, last_sum, head_sum, up_sum)
    grad_input = grad_input.reshape(shards, group, span, width)
    grad_tokens = to_positions(send_back(grad_input.astype(bf16)), me)
    cur = jnp.sum(grad_input, axis=1)
    bit = 1
    while cur.shape[0] > 1:
        halves = cur.reshape(cur.shape[0] // 2, 2, span, width)
        cur = halves[:, 0] + swap(halves[:, 1].astype(bf16), "seq", bit).astype(f32)
        cur = tie(cur, last_sum, head_sum, up_sum)
        bit *= 2
    pieces = lax.axis_size("dp")
    cur = cur[0].astype(bf16).reshape(span, pieces, width // pieces).transpose(1, 0, 2)
    bits = [1 << b for b in range(pieces.bit_length() - 1)]
    for n, bit in enumerate(bits):
        mine = (lax.axis_index("dp") // bit) % 2
        halves = cur.reshape(cur.shape[0] // 2, 2, span, width // pieces)
        keep = lax.dynamic_index_in_dim(halves, mine, 1, keepdims=False)
        send = lax.dynamic_index_in_dim(halves, 1 - mine, 1, keepdims=False)
        total = keep.astype(f32) + swap(send, "dp", bit).astype(f32)
        cur = total if n + 1 == len(bits) else total.astype(bf16)
        if last_sum.left:
            cur = tie(cur, last_sum, head_sum)
    grad_pos = cur.reshape(span, width // pieces)

    grad_w_up = up_sum.finish()
    head_part = head_sum.finish()
    grad_w_out = head_part[:, first.shape[1] :]
    head_part = split(head_part[:, : first.shape[1]], 1)
    last_part = last_sum.finish()
    small = last_part[:, last.shape[1] :].T
    last_part = split(last_part[:, : last.shape[1]], 1)
    grad_w_qkv = jnp.concatenate([x for pair in zip(head_part, last_part) for x in pair], axis=1)
    rest = len(vectors)
    wide_up = small[rest : rest + ups].reshape(-1)
    norms = small[rest + ups : rest + ups + lines].reshape(-1)
    norm_values = jnp.sqrt(norms[:5] / (norms[5] * width))
    return (
        mixed_out,
        grad_tokens,
        norm_values,
        grad_pos,
        grad_w_qkv,
        small[0],
        small[1],
        grad_w_out,
        small[2],
        small[3],
        small[4],
        grad_w_up,
        wide_up,
        grad_w_down,
        small[5],
        small[6],
        small[7],
    )


def solution(mesh):
    in_specs = (
        P("dp", "seq", None),
        P("dp", "seq", None),
        P("dp"),
        P("dp", "seq"),
        P("dp", "seq"),
        P("seq", None),
    ) + (P(),) * 13
    both = ("dp", "seq")
    out_specs = (
        P("dp", "seq", None),
        P("dp", "seq", None),
        P(),
        P("seq", "dp"),
        P(both, None),
        P(both),
        P(both),
        P(both, None),
        P(both),
        P(both),
        P(both),
        P(both, None),
        P(both),
        P(both, None),
        P(both),
        P(both),
        P(both),
    )
    return jax.shard_map(local, mesh=mesh, in_specs=in_specs, out_specs=out_specs, check_vma=False)
```

```python
import math

import jax
import jax.numpy as jnp
from jax import lax
from jax.experimental import pallas as pl
from jax.experimental.pallas import tpu as pltpu
from jax.sharding import PartitionSpec as P

H = 12
HD = 64
PAIR = 2 * HD
INTERPRET = False


norm_eps = 1e-12
f32 = jnp.float32
bf16 = jnp.bfloat16
NT = (((1,), (1,)), ((), ()))
TN = (((0,), (0,)), ((), ()))
NN = (((1,), (0,)), ((), ()))


def mm(a, b, dims=NN):
    return lax.dot_general(a, b, dims, preferred_element_type=f32)


def probs_of(q, k, bias):
    s = mm(k, q * (1.0 / math.sqrt(HD)), NT) + bias
    e = jnp.exp(s - jnp.max(s, axis=0, keepdims=True))
    return e, 1.0 / jnp.sum(e, axis=0, keepdims=True)


def rows_of(ref, cols=slice(None)):
    blocks = [ref[i, 0, :, cols] for i in range(ref.shape[0])]
    return jnp.concatenate(blocks, axis=0)


def put_rows(ref, value, cols=slice(None)):
    span = ref.shape[2]
    for i in range(ref.shape[0]):
        ref[i, 0, :, cols] = value[i * span : (i + 1) * span]


def wide_bias(bias_ref):
    bias = rows_of(bias_ref)
    return jnp.concatenate([bias] * (bias.shape[0] // 128), axis=1)


def attend_kernel(q_ref, k_ref, v_ref, bias_ref, out_ref):
    bias = wide_bias(bias_ref)
    parts = []
    for i in range(2):
        cols = slice(i * HD, (i + 1) * HD)
        e, inv = probs_of(rows_of(q_ref, cols), rows_of(k_ref, cols), bias)
        parts.append(mm(rows_of(v_ref, cols), (e * inv).astype(bf16), TN))
    put_rows(out_ref, jnp.concatenate(parts, axis=0).T.astype(bf16))


def attend_back_kernel(q_ref, k_ref, v_ref, bias_ref, g_ref, out_ref):
    bias = wide_bias(bias_ref)
    scale = 1.0 / math.sqrt(HD)
    dq, dk, dv = [], [], []
    for i in range(2):
        cols = slice(i * HD, (i + 1) * HD)
        q, k, v, g = (rows_of(ref, cols) for ref in (q_ref, k_ref, v_ref, g_ref))
        e, inv = probs_of(q, k, bias)
        p = e * inv
        t = p * mm(v, g, NT)
        ds = (t - p * jnp.sum(t, axis=0, keepdims=True)).astype(bf16)
        dv.append(mm(p.astype(bf16), g))
        dk.append(mm(ds, q * scale))
        dq.append(mm(k, ds, TN) * scale)
    grads = (
        jnp.concatenate(dq, axis=0).T.astype(bf16),
        jnp.concatenate(dk, axis=1).astype(bf16),
        jnp.concatenate(dv, axis=1).astype(bf16),
    )
    pairs = out_ref.shape[3] // (3 * PAIR)
    for j in range(pairs):

        @pl.when(pl.program_id(1) == j)
        def _():
            for part, grad in enumerate(grads):
                at = (part * pairs + j) * PAIR
                put_rows(out_ref, grad, slice(at, at + PAIR))


def pair_spec(shape, off):
    return pl.BlockSpec((shape[0], 1, shape[2], PAIR), lambda b, h: (0, b, 0, off + h))


def bias_spec(shape):
    return pl.BlockSpec((shape[0], 1, shape[2], 128), lambda b, h: (0, b, 0, 0))


def attend(projected, bias):
    shape = projected.shape
    pairs = shape[3] // (3 * PAIR)
    return pl.pallas_call(
        attend_kernel,
        grid=(shape[1], pairs),
        in_specs=[pair_spec(shape, i * pairs) for i in range(3)] + [bias_spec(shape)],
        out_specs=pair_spec(shape, 0),
        out_shape=jax.ShapeDtypeStruct(shape[:3] + (shape[3] // 3,), bf16),
        interpret=INTERPRET,
        name="attend",
    )(projected, projected, projected, bias)


def attend_back(projected, bias, grad_context, first, take):
    shape = projected.shape
    pairs = shape[3] // (3 * PAIR)
    wide = 3 * take * PAIR
    return pl.pallas_call(
        attend_back_kernel,
        grid=(shape[1], take),
        in_specs=[pair_spec(shape, i * pairs + first) for i in range(3)]
        + [bias_spec(shape), pair_spec(shape, first)],
        out_specs=pl.BlockSpec((shape[0], 1, shape[2], wide), lambda b, h: (0, b, 0, 0)),
        out_shape=jax.ShapeDtypeStruct(shape[:3] + (wide,), bf16),
        interpret=INTERPRET,
        name="attend_back",
    )(projected, projected, projected, bias, grad_context)


def swap(value, axis, bits):
    size = lax.axis_size(axis)
    return lax.ppermute(value, axis, [(i, i ^ bits) for i in range(size)])


class Halving:
    def __init__(self, values, order):
        dims = []
        for axis in ("dp", "seq"):
            count = lax.axis_size(axis).bit_length() - 1
            dims += [(axis, 1 << b) for b in reversed(range(count))]
        self.cur = values.reshape((2,) * len(dims) + values.shape[1:])
        self.dims = dims
        self.left = [d for d in order if d in dims] + [d for d in dims[::-1] if d not in order]

    def step(self):
        if not self.left:
            return
        bit = self.left.pop(0)
        at = self.dims.index(bit)
        self.dims.pop(at)
        mine = (lax.axis_index(bit[0]) // bit[1]) % 2
        keep = lax.dynamic_index_in_dim(self.cur, mine, at, keepdims=False)
        send = lax.dynamic_index_in_dim(self.cur, 1 - mine, at, keepdims=False)
        total = keep.astype(f32) + swap(send, bit[0], bit[1]).astype(f32)
        self.cur = total.astype(self.cur.dtype) if self.left else total

    def finish(self):
        while self.left:
            self.step()
        return self.cur


def tie(value, *chains):
    value, held = lax.optimization_barrier((value, [c.cur for c in chains]))
    for chain, cur in zip(chains, held):
        chain.cur = cur
        chain.step()
    return value


CORE, XBIT = ("seq", 1), ("seq", 2)
YBIT, ZLOW, ZHIGH = ("dp", 1), ("dp", 2), ("dp", 4)
UP_PATH = (CORE, ZLOW, YBIT, ZHIGH, XBIT)
HEAD_PATH = (CORE, YBIT, ZLOW, XBIT, ZHIGH)
LAST_PATH = (CORE, ZLOW, YBIT, XBIT, ZHIGH)


def to_sequences(value, shards, me):
    group = value.shape[0] // shards

    def block(r):
        return lax.dynamic_slice_in_dim(value, (me ^ r) * group, group, 0)

    parts = [block(0)] + [swap(block(r), "seq", r) for r in range(1, shards)]
    return jnp.concatenate(parts, axis=0)


def send_back(value):
    return [value[0]] + [swap(value[r], "seq", r) for r in range(1, value.shape[0])]


def to_positions(parts, me):
    group = parts[0].shape[0]
    out = jnp.zeros((group * len(parts),) + parts[0].shape[1:], parts[0].dtype)
    for r, part in enumerate(parts):
        out = lax.dynamic_update_slice_in_dim(out, part, (me ^ r) * group, 0)
    return out


def normalize(values):
    centred = values - jnp.mean(values, axis=-1, keepdims=True)
    spread = lax.rsqrt(jnp.mean(centred * centred, axis=-1, keepdims=True) + norm_eps)
    return centred * spread, spread


def normalize_back(grad, normed, spread, gain):
    scaled = grad * gain
    return spread * (
        scaled
        - jnp.mean(scaled, axis=-1, keepdims=True)
        - normed * jnp.mean(scaled * normed, axis=-1, keepdims=True)
    )


def local(
    tokens,
    cotangent,
    lengths,
    mlm_mask,
    token_weight,
    pos_table,
    w_qkv,
    b_query,
    b_value,
    w_out,
    b_out,
    gain_attn,
    shift_attn,
    w_up,
    b_up,
    w_down,
    b_down,
    gain_out,
    shift_out,
):
    rows, span, width = tokens.shape
    shards = lax.axis_size("seq")
    devices = shards * lax.axis_size("dp")
    me = lax.axis_index("seq")
    group = rows // shards
    count = group * span * shards

    positions = me * span + lax.iota(jnp.int32, span)
    valid_here = (positions[None, :] < lengths[:, None]).astype(f32)
    resid_here = tokens.astype(f32) + pos_table.astype(f32)[None]
    square_in = jnp.sum(valid_here[..., None] * resid_here * resid_here)
    flat = to_sequences(resid_here.astype(bf16), shards, me).reshape(count, width)
    marks = to_sequences(token_weight * 2 + mlm_mask, shards, me).reshape(shards, group, span)
    flat, cotangent = lax.optimization_barrier((flat, cotangent))
    cot = to_sequences(cotangent, shards, me)
    my_lengths = lax.dynamic_slice_in_dim(lengths, me * group, group, 0)
    order = jnp.stack([(me ^ r) * span + lax.iota(jnp.int32, span) for r in range(shards)])
    live = order[:, None, :] < my_lengths[None, :, None]
    valid_mask = live.astype(f32)
    bias = jnp.broadcast_to(
        jnp.where(live, 0.0, -jnp.inf).astype(f32)[..., None], (shards, group, span, 128)
    )
    picked = valid_mask * (marks % 2).astype(f32)
    masked_count = jnp.sum(picked, axis=(0, 2), keepdims=True)
    weighting = (
        valid_mask
        * (marks // 2).astype(f32)
        * (
            1.0
            + picked * my_lengths.astype(f32)[None, :, None] / jnp.maximum(masked_count, 1.0)
        )
        * 0.125
    )
    mask_column = valid_mask.reshape(count, 1)

    bias_full = jnp.concatenate(
        [b_query.astype(f32), jnp.zeros((width,), f32), b_value.astype(f32)]
    )
    projected = (mm(flat, w_qkv) + bias_full).astype(bf16).reshape(shards, group, span, 3 * width)
    context = attend(projected, bias).reshape(count, width)
    context, cot = lax.optimization_barrier((context, cot))
    attn_out = mm(context, w_out) + b_out.astype(f32)
    n_one, r_one = normalize(flat.astype(f32) + attn_out)
    gain_one = gain_attn.astype(f32)
    normed_one = n_one * gain_one + shift_attn.astype(f32)
    ffn_in = normed_one.astype(bf16)
    hidden_pre = mm(ffn_in, w_up) + b_up.astype(f32)
    below = 0.5 * (1.0 + lax.erf(hidden_pre * math.sqrt(0.5)))
    density = jnp.exp(-0.5 * hidden_pre * hidden_pre) * (1.0 / math.sqrt(2.0 * math.pi))
    hidden_act = (hidden_pre * below).astype(bf16)
    slope = (below + hidden_pre * density).astype(bf16)
    ffn_out = mm(hidden_act, w_down) + b_down.astype(f32)
    n_two, r_two = normalize(normed_one + ffn_out)
    gain_two = gain_out.astype(f32)
    normed_two = n_two * gain_two + shift_out.astype(f32)
    mixed_parts = send_back(normed_two.astype(bf16).reshape(shards, group, span, width))
    norms = jnp.stack(
        [square_in]
        + [jnp.sum(mask_column * m * m) for m in (normed_one, normed_two, attn_out, ffn_out)]
        + [jnp.sum(valid_mask)]
    )

    def spread_rows(g):
        return g.astype(bf16).reshape(devices, g.shape[0] // devices, g.shape[1])

    grad_two = cot.reshape(count, width).astype(f32) * weighting.reshape(count, 1)
    grad_gain_out = jnp.sum(grad_two * n_two, axis=0)
    grad_shift_out = jnp.sum(grad_two, axis=0)
    grad_resid_two = normalize_back(grad_two, n_two, r_two, gain_two)
    grad_ffn = grad_resid_two.astype(bf16)
    grad_b_down = jnp.sum(grad_ffn, axis=0, dtype=f32)
    down_part = mm(hidden_act, grad_ffn, TN).astype(bf16)
    grad_ffn, down_part = lax.optimization_barrier((grad_ffn, down_part))
    grad_w_down = lax.psum_scatter(down_part, ("dp", "seq"), scatter_dimension=0, tiled=True)
    grad_w_down = grad_w_down.astype(f32)
    grad_pre = (mm(grad_ffn, w_down, NT) * slope.astype(f32)).astype(bf16)
    grad_b_up = jnp.sum(grad_pre, axis=0, dtype=f32)
    up_sum = Halving(spread_rows(mm(ffn_in, grad_pre, TN)), UP_PATH)
    grad_pre = tie(grad_pre, up_sum)
    grad_one = grad_resid_two + mm(grad_pre, w_up, NT)
    grad_one = tie(grad_one, up_sum)
    grad_gain_attn = jnp.sum(grad_one * n_one, axis=0)
    grad_shift_attn = jnp.sum(grad_one, axis=0)
    grad_resid_one = normalize_back(grad_one, n_one, r_one, gain_one)
    grad_attn = grad_resid_one.astype(bf16)
    grad_b_out = jnp.sum(grad_attn, axis=0, dtype=f32)
    out_part = mm(context, grad_attn, TN).astype(bf16)
    grad_context = mm(grad_attn, w_out, NT).astype(bf16).reshape(shards, group, span, width)
    grad_context, mixed_parts = lax.optimization_barrier((grad_context, mixed_parts))
    mixed_out = to_positions(mixed_parts, me)

    pairs = width // PAIR
    takes = (pairs - pairs // 3, pairs // 3)
    first = attend_back(projected, bias, grad_context, 0, takes[0]).reshape(count, -1)
    head_part = jnp.concatenate([mm(flat, first, TN).astype(bf16), out_part], axis=1)
    head_sum = Halving(spread_rows(head_part), HEAD_PATH)
    grad_context = tie(grad_context, head_sum)
    last = attend_back(projected, bias, grad_context, takes[0], takes[1]).reshape(count, -1)
    last = tie(last, up_sum, head_sum)
    first_sum = jnp.sum(first, axis=0, dtype=f32)
    last_sum = jnp.sum(last, axis=0, dtype=f32)

    def split(values, axis):
        return jnp.split(values, 3, axis=axis)

    (q_first, _, v_first), (q_last, _, v_last) = split(first_sum, 0), split(last_sum, 0)
    each = width // devices
    vectors = [
        jnp.concatenate([q_first, q_last]),
        jnp.concatenate([v_first, v_last]),
        grad_b_out,
        grad_gain_attn,
        grad_shift_attn,
        grad_b_down,
        grad_gain_out,
        grad_shift_out,
    ]
    ups = grad_b_up.shape[0] // width
    lines = -(-norms.shape[0] // each)
    norms = jnp.pad(norms, (0, lines * each - norms.shape[0])).reshape(lines, each)
    table = jnp.concatenate(
        [v[None] for v in vectors]
        + [
            grad_b_up.reshape(devices, ups, each).transpose(1, 0, 2).reshape(ups, width),
            jnp.tile(norms, (1, devices)),
        ],
        axis=0,
    )
    table = jnp.pad(table, ((0, 128 - table.shape[0]), (0, 0))).T
    last_grad = jnp.concatenate([mm(flat, last, TN).astype(bf16), table.astype(bf16)], axis=1)
    last_sum = Halving(spread_rows(last_grad), LAST_PATH)
    last = tie(last, last_sum)
    cut = takes[0] * PAIR

    def columns(lo, hi):
        return [w_qkv[:, i * width + lo : i * width + hi] for i in range(3)]

    w_first = jnp.concatenate(columns(0, cut), axis=1)
    w_last = jnp.concatenate(columns(cut, width), axis=1)
    grad_input = grad_resid_one + mm(first, w_first, NT) + mm(last, w_last, NT)
    grad_input = tie(grad_input, last_sum, head_sum, up_sum)
    grad_input = grad_input.reshape(shards, group, span, width)
    grad_tokens = to_positions(send_back(grad_input.astype(bf16)), me)
    cur = jnp.sum(grad_input, axis=1)
    bit = 1
    while cur.shape[0] > 1:
        halves = cur.reshape(cur.shape[0] // 2, 2, span, width)
        cur = halves[:, 0] + swap(halves[:, 1].astype(bf16), "seq", bit).astype(f32)
        cur = tie(cur, last_sum, head_sum, up_sum)
        bit *= 2
    pieces = lax.axis_size("dp")
    cur = cur[0].astype(bf16).reshape(span, pieces, width // pieces).transpose(1, 0, 2)
    bits = [1 << b for b in range(pieces.bit_length() - 1)]
    for n, bit in enumerate(bits):
        mine = (lax.axis_index("dp") // bit) % 2
        halves = cur.reshape(cur.shape[0] // 2, 2, span, width // pieces)
        keep = lax.dynamic_index_in_dim(halves, mine, 1, keepdims=False)
        send = lax.dynamic_index_in_dim(halves, 1 - mine, 1, keepdims=False)
        total = keep.astype(f32) + swap(send, "dp", bit).astype(f32)
        cur = total if n + 1 == len(bits) else total.astype(bf16)
        if last_sum.left:
            cur = tie(cur, last_sum, head_sum)
    grad_pos = cur.reshape(span, width // pieces)

    grad_w_up = up_sum.finish()
    head_part = head_sum.finish()
    grad_w_out = head_part[:, first.shape[1] :]
    head_part = split(head_part[:, : first.shape[1]], 1)
    last_part = last_sum.finish()
    small = last_part[:, last.shape[1] :].T
    last_part = split(last_part[:, : last.shape[1]], 1)
    grad_w_qkv = jnp.concatenate([x for pair in zip(head_part, last_part) for x in pair], axis=1)
    rest = len(vectors)
    wide_up = small[rest : rest + ups].reshape(-1)
    norms = small[rest + ups : rest + ups + lines].reshape(-1)
    norm_values = jnp.sqrt(norms[:5] / (norms[5] * width))
    return (
        mixed_out,
        grad_tokens,
        norm_values,
        grad_pos,
        grad_w_qkv,
        small[0],
        small[1],
        grad_w_out,
        small[2],
        small[3],
        small[4],
        grad_w_up,
        wide_up,
        grad_w_down,
        small[5],
        small[6],
        small[7],
    )


def solution(mesh):
    in_specs = (
        P("dp", "seq", None),
        P("dp", "seq", None),
        P("dp"),
        P("dp", "seq"),
        P("dp", "seq"),
        P("seq", None),
    ) + (P(),) * 13
    both = ("dp", "seq")
    out_specs = (
        P("dp", "seq", None),
        P("dp", "seq", None),
        P(),
        P("seq", "dp"),
        P(both, None),
        P(both),
        P(both),
        P(both, None),
        P(both),
        P(both),
        P(both),
        P(both, None),
        P(both),
        P(both, None),
        P(both),
        P(both),
        P(both),
    )
    return jax.shard_map(local, mesh=mesh, in_specs=in_specs, out_specs=out_specs, check_vma=False)
```
